128 devices in a mesh: outer: 8 (over z, core), inner: 16 (over y, x).
Axes of the slice: x: 4, y: 4, z: 4, core: 2. Of those that a mesh axis runs over, the one named last changes fastest.
Arguments:
- queries: bfloat16 [131072, 2048], P(('outer', 'inner')), may hold values from -6 to 6
- keys: bfloat16 [131072, 2048], P(('outer', 'inner')), may hold values from -6 to 6
- values: bfloat16 [131072, 2048], P(('outer', 'inner')), may hold values from -6 to 6
- level_weights: float32 [12, 32], replicated, may hold values from 0.1 to 1
- out_weight: bfloat16 [2048, 2048], replicated, may hold values from -0.125 to 0.125
Outputs:
- mixed_out: bfloat16 [131072, 2048], P(('outer', 'inner'))
The draws below stay inside these ranges and needn't reach their ends.
All inputs are finite; a program needn't handle non-finite values.
Results may differ from the reference program's by a relative error of at most 0.0071.
Values sent between devices are 32-bit elements; how exact they have to be, the bound alone decides.
No kernel may reach another device: no remote copies, remote signals or barrier semaphores. Data moves between devices by JAX's collectives and lax.ppermute only.
A program may use at most 256 MiB of HBM per device.

```python
import math
import jax
import jax.numpy as jnp
import numpy as np
from jax import lax

D = 2048
H = 32
SPAN = 64
TOK_DEV = 1024
TOKENS = 131072
LEVELS = 12


def steps_of(key, dims, cuts, smallest, largest):
    factor_of = 1.0
    for axis_at, parts in cuts:
        draws = jax.random.uniform(jax.random.fold_in(jax.random.fold_in(key, 6), axis_at), (parts,), jnp.float32, smallest / len(cuts), largest / len(cuts))
        factor_of = factor_of * jnp.repeat(jnp.exp(draws), dims[axis_at] // parts).reshape((-1,) + (1,) * (len(dims) - 1 - axis_at))
    return factor_of


def scatter_about(rng, extent, spread, most, shards=(), kind=jnp.bfloat16):
    values = jax.random.normal(rng, extent, jnp.float32) * spread
    if len(shards) > 0:
        values = steps_of(rng, extent, shards, -0.22, 0.18) * values
    return jnp.clip(values, min=-most, max=most).astype(kind)


def setup_inputs(seed: int = 0) -> dict:
    key_of = jax.random.split(jax.random.key(seed), 6)
    return {
        "queries": scatter_about(key_of[0], (TOKENS, D), 1.0, 6.0, ((0, 128),)),
        "keys": scatter_about(key_of[1], (TOKENS, D), 1.0, 6.0, ((0, 128),)),
        "values": scatter_about(key_of[2], (TOKENS, D), 1.0, 6.0, ((0, 128),)),
        "level_weights": jnp.clip(jnp.exp(jax.random.uniform(key_of[3], (LEVELS, H), jnp.float32, math.log(0.1), math.log(1.0))), 0.1, 1.0),
        "out_weight": scatter_about(key_of[4], (D, D), D ** -0.5, 0.125),
    }


def level_table(count, levels, head_dim, span):
    table = np.zeros((count, count, levels), np.float32)
    for later in range(count):
        for early in range(later):
            level = (early ^ later).bit_length()
            table[later, early, level] = math.sqrt(head_dim / (span * 2 ** (level - 1)))
    return table

def unit_heads(source, heads, span):
    rows, width = source.shape
    scaled = source.reshape(rows // span, span, heads, width // heads).astype(jnp.float32)
    scaled = scaled * lax.rsqrt(lax.optimization_barrier(jnp.sum(scaled * scaled, axis=-1, keepdims=True)) + 1e-06)
    return scaled.astype(jnp.bfloat16)

def block_mix(queries, keys, values, level_weights, tree):
    heads = level_weights.shape[1]
    head_dim = queries.shape[1] // heads
    q_unit = unit_heads(queries, heads, SPAN).astype(jnp.float32)
    k_unit = unit_heads(keys, heads, SPAN).astype(jnp.float32)
    v_heads = values.reshape(q_unit.shape).astype(jnp.float32)
    count = q_unit.shape[0]
    states = jnp.einsum('cthd,cthe->chde', k_unit, v_heads).reshape(count, heads, head_dim * head_dim)
    table = jnp.asarray(level_table(count, level_weights.shape[0], head_dim, SPAN), level_weights.dtype)
    coeffs = jnp.einsum('jil,lh->hji', table, level_weights, precision=lax.Precision.HIGHEST)
    local = jnp.einsum('hji,ihf->jhf', coeffs, states, precision=lax.Precision.HIGHEST)
    merged = (local + tree[None]).astype(jnp.bfloat16).reshape(count, heads, head_dim, head_dim)
    scores = jnp.einsum('cthd,cshd->chts', q_unit, k_unit)
    causal = jnp.tril(jnp.ones((SPAN, SPAN), bool))
    factor = level_weights[0] * math.sqrt(head_dim / SPAN)
    weights = jnp.where(causal, scores * factor[None, :, None, None], 0.0).astype(jnp.bfloat16)
    mixed = jnp.einsum('chts,cshd->cthd', weights.astype(jnp.float32), v_heads)
    mixed = mixed + jnp.einsum('cthd,chde->cthe', q_unit, merged.astype(jnp.float32))
    return (lax.optimization_barrier(jnp.sum(states, axis=0)), mixed.astype(jnp.bfloat16).reshape(queries.shape))

def reference(queries, keys, values, level_weights, out_weight):
    blocks = TOKENS // TOK_DEV
    depth = blocks.bit_length() - 1
    local_levels = (TOK_DEV // SPAN).bit_length() - 1
    heads = level_weights.shape[1]
    head_dim = D // heads
    scales = np.array([math.sqrt(head_dim / (SPAN * 2 ** (local_levels + step))) for step in range(depth)], np.float32)
    factors = level_weights[local_levels + 1:local_levels + 1 + depth] * jnp.asarray(scales, level_weights.dtype)[:, None]
    steps_idx = jnp.arange(depth, dtype=jnp.int32)

    def advance(carry, inputs):
        current, finished, index = carry
        q_block, k_block, v_block = inputs
        taken = (index >> steps_idx & 1).astype(jnp.float32)
        tree = jnp.einsum('m,mh,mhf->hf', taken, factors, finished, precision=lax.Precision.HIGHEST)
        total, mixed = block_mix(q_block, k_block, v_block, level_weights, tree)
        current = current + total[None]
        closes = (index + 1) % jnp.left_shift(jnp.int32(1), steps_idx) == 0
        finished = jnp.where(closes[:, None, None], current, finished)
        current = jnp.where(closes[:, None, None], 0.0, current)
        return ((current, finished, index + 1), mixed)
    start = jnp.zeros((depth, heads, head_dim * head_dim), jnp.float32)
    shaped = (queries.reshape(blocks, TOK_DEV, D), keys.reshape(blocks, TOK_DEV, D), values.reshape(blocks, TOK_DEV, D))
    carry, mixed = lax.scan(advance, (start, start, jnp.int32(0)), shaped)
    mixed = mixed.reshape(TOKENS, D)
    return jnp.dot(mixed, out_weight, preferred_element_type=jnp.float32).astype(jnp.bfloat16)
```

```python
import functools
import math

import jax
import jax.numpy as jnp
from jax import lax
from jax.experimental import pallas as pl
from jax.experimental.pallas import tpu as pltpu
from jax.sharding import PartitionSpec as P

SPAN = 64
LANES = 128
WIDE = 256
PIECES = (2, 2, 1, 2, 1)
TOTALS_WIDE = 512
INSIDE_MIB = 32
FINISH_MIB = 40
EPS = 1e-06


def in_hbm(array):
    return pltpu.with_memory_space_constraint(array, pltpu.HBM)


def mib(count):
    return count * 1024 * 1024


def same_head(size, kind):
    row = lax.broadcasted_iota(jnp.int32, (size, size), 0) // SPAN
    col = lax.broadcasted_iota(jnp.int32, (size, size), 1) // SPAN
    return jnp.where(row == col, 1.0, 0.0).astype(kind)


def inverse_norm(block):
    total = jnp.dot(
        block * block, same_head(block.shape[1], block.dtype), preferred_element_type=jnp.float32
    )
    return lax.rsqrt(total + EPS)


def scaled(block, factor):
    return (block.astype(jnp.float32) * factor).astype(jnp.bfloat16)


def pair_state(keys, values):
    both = lax.dot_general(
        keys, values, (((0,), (0,)), ((), ())), preferred_element_type=jnp.float32
    )
    lane = lax.broadcasted_iota(jnp.int32, (SPAN, LANES), 1)
    return jnp.where(lane < SPAN, both[:SPAN], both[SPAN:])


def by_head(block, low):
    zero = jnp.zeros_like(block)
    return jnp.concatenate([jnp.where(low, block, zero), jnp.where(low, zero, block)], axis=0)


def totals_kernel(where_ref, k_ref, v_ref, kn_ref, *outs):
    *outs, held = outs
    step = pl.program_id(0)
    pairs = k_ref.shape[1] // LANES
    factors = [inverse_norm(k_ref[:, at : at + WIDE]) for at in range(0, k_ref.shape[1], WIDE)]
    for group, factor in enumerate(factors):
        cut = slice(group * WIDE, (group + 1) * WIDE)
        kn_ref[:, cut] = scaled(k_ref[:, cut], factor)
    states = []
    for pair in range(pairs):
        cut = slice(pair * LANES, (pair + 1) * LANES)
        states.append(pair_state(kn_ref[:, cut], v_ref[:, cut]))
    for pair, state in enumerate(states):
        held[step * pairs + pair] = state

    @pl.when(step == pl.num_programs(0) - 1)
    def _():
        for index, out in enumerate(outs):
            first = (where_ref[0] ^ index) * 4
            for pair in range(4):
                out[pair] = held[first + pair]


def device_totals(place, keys, values):
    rows, width = keys.shape
    step_width = TOTALS_WIDE
    steps = width // step_width
    block = pl.BlockSpec((rows, step_width), lambda i, s: (0, i))
    whole = pl.BlockSpec((4, SPAN, LANES), lambda i, s: (0, 0, 0))
    return pl.pallas_call(
        totals_kernel,
        out_shape=[pltpu.HBM(keys.shape, keys.dtype)]
        + [jax.ShapeDtypeStruct((4, SPAN, LANES), jnp.float32)] * 4,
        grid_spec=pltpu.PrefetchScalarGridSpec(
            num_scalar_prefetch=1,
            grid=(steps,),
            in_specs=[block, block],
            out_specs=[block] + [whole] * 4,
            scratch_shapes=[pltpu.VMEM((width // LANES, SPAN, LANES), jnp.float32)],
        ),
        compiler_params=pltpu.CompilerParams(vmem_limit_bytes=mib(32)),
        cost_estimate=pl.CostEstimate(
            flops=4 * rows * width * WIDE, bytes_accessed=6 * rows * width, transcendentals=0
        ),
        name="totals",
    )(place, keys, values)


def two_span_states(keys, values):
    zero = jnp.zeros((SPAN, LANES), values.dtype)
    spread = jnp.concatenate(
        [
            jnp.concatenate([values[:SPAN], zero], axis=1),
            jnp.concatenate([zero, values[SPAN:]], axis=1),
        ],
        axis=0,
    )
    both = lax.dot_general(
        keys, spread, (((0,), (0,)), ((), ())), preferred_element_type=jnp.float32
    )
    lane = lax.broadcasted_iota(jnp.int32, (SPAN, LANES), 1)
    return [
        jnp.where(lane < SPAN, both[:SPAN, at : at + LANES], both[SPAN:, at : at + LANES])
        for at in (0, LANES)
    ]


def inside_kernel(w_ref, q_ref, k_ref, v_ref, *refs):
    y_ref, qn_ref, seen_ref = refs[-3:]
    rows = q_ref.shape[0]
    spans = rows // SPAN
    query = q_ref[...]
    query = scaled(query, inverse_norm(query))
    qn_ref[...] = query
    lane = lax.broadcasted_iota(jnp.int32, (SPAN, LANES), 1)
    low = lane < SPAN
    seen = (lane % SPAN) <= lax.broadcasted_iota(jnp.int32, (SPAN, LANES), 0)
    pairs = [slice(at, at + LANES) for at in range(0, q_ref.shape[1], LANES)]
    parts = [slice(c * SPAN, (c + 1) * SPAN) for c in range(spans)]
    states = [
        sum(
            (
                two_span_states(k_ref[at : at + 2 * SPAN, cut], v_ref[at : at + 2 * SPAN, cut])
                for at in range(0, rows, 2 * SPAN)
            ),
            [],
        )
        for cut in pairs
    ]
    for pair, cut in enumerate(pairs):
        factor = jnp.where(seen, w_ref[pair][0:1], 0.0)
        for part in parts:
            scores = lax.dot_general(
                qn_ref[part, cut],
                by_head(k_ref[part, cut], low),
                (((1,), (1,)), ((), ())),
                preferred_element_type=jnp.float32,
            )
            seen_ref[part, cut] = (scores * factor).astype(jnp.bfloat16)
    mixes = []
    for pair in range(len(pairs)):
        weight = w_ref[pair]
        level = states[pair]
        mix = [None] * spans
        for bit in range(spans.bit_length() - 1):
            size = 1 << bit
            for node in range(0, len(level), 2):
                term = level[node] * weight[1 + bit : 2 + bit]
                for c in range((node + 1) * size, (node + 2) * size):
                    mix[c] = term if mix[c] is None else mix[c] + term
            level = [level[n] + level[n + 1] for n in range(0, len(level), 2)]
        mixes.append(mix)
    for pair, cut in enumerate(pairs):
        for c, part in enumerate(parts):
            left = seen_ref[part, cut]
            right = by_head(v_ref[part, cut], low)
            if c > 0:
                left = jnp.concatenate([left, qn_ref[part, cut]], axis=1)
                right = jnp.concatenate(
                    [right, by_head(mixes[pair][c].astype(jnp.bfloat16), low)], axis=0
                )
            y_ref[part, cut] = jnp.dot(left, right, preferred_element_type=jnp.float32).astype(
                jnp.bfloat16
            )


def inside(weights, queries, keys, values, piece, so_far):
    rows, width = queries.shape
    steps = PIECES[piece]
    start = sum(PIECES[:piece])
    block = pl.BlockSpec((rows, WIDE), lambda i: (0, start + i))
    table = pl.BlockSpec((2, 16, LANES), lambda i: (start + i, 0, 0))
    count = len(so_far)
    return pl.pallas_call(
        inside_kernel,
        out_shape=[pltpu.HBM((rows, width), jnp.bfloat16)] * 2,
        grid_spec=pltpu.PrefetchScalarGridSpec(
            num_scalar_prefetch=0,
            grid=(steps,),
            in_specs=[table, block, block, block] + [pl.BlockSpec(memory_space=pl.ANY)] * count,
            out_specs=[block, block],
            scratch_shapes=[pltpu.VMEM((rows, WIDE), jnp.bfloat16)],
        ),
        input_output_aliases={4 + n: n for n in range(count)},
        compiler_params=pltpu.CompilerParams(vmem_limit_bytes=mib(INSIDE_MIB)),
        cost_estimate=pl.CostEstimate(
            flops=16 * rows * WIDE * steps * WIDE,
            bytes_accessed=10 * rows * WIDE * steps,
            transcendentals=0,
        ),
        name="inside",
    )(weights, queries, keys, values, *so_far)


def finish_kernel(where_ref, y_ref, q_ref, *refs):
    trees = refs[:4]
    w_ref, out_ref, left, total = refs[4:]
    step = pl.program_id(0)

    @pl.when(step <= 3)
    def _():
        low = lax.broadcasted_iota(jnp.int32, (SPAN, LANES), 1) < SPAN
        blocks = []
        for slot in range(4):
            tree = trees[0][slot]
            for m in range(1, 4):
                tree = jnp.where(step == m, trees[m][slot], tree)
            tree = by_head(tree.astype(jnp.bfloat16), low)
            zero = jnp.zeros_like(tree)
            blocks.append(jnp.concatenate([tree, zero] if slot % 2 == 0 else [zero, tree], axis=1))
        for group in range(2):
            cut = slice(group * WIDE, (group + 1) * WIDE)
            mixed = y_ref[:, cut].astype(jnp.float32) + jnp.dot(
                q_ref[:, cut],
                jnp.concatenate(blocks[2 * group : 2 * group + 2], axis=0),
                preferred_element_type=jnp.float32,
            )
            left[:, cut] = mixed.astype(jnp.bfloat16)

    def product(cut):
        return jnp.dot(left[...], w_ref[:, cut], preferred_element_type=jnp.float32)

    @pl.when(step == 0)
    def _():
        for n in range(total.shape[0]):
            total[n] = product(slice(n * WIDE, (n + 1) * WIDE))

    @pl.when((step > 0) & (step < 3))
    def _():
        for n in range(total.shape[0]):
            total[n] += product(slice(n * WIDE, (n + 1) * WIDE))

    @pl.when(step >= 3)
    def _():
        n = jnp.maximum(step - 3, 0)
        cut = pl.ds(pl.multiple_of(n * WIDE, WIDE), WIDE)
        out_ref[...] = (total[n] + product(cut)).astype(jnp.bfloat16)


def finish(place, mixed, query, trees, out_weight):
    rows = mixed.shape[0]
    width = out_weight.shape[0]
    quarter = width // 4
    first = pl.BlockSpec((rows, quarter), lambda i, s: (0, jnp.minimum(i, 3) ^ s[0]))
    tree = pl.BlockSpec((4, SPAN, LANES), lambda i, s: (0, 0, 0), pipeline_mode=pl.Buffered(1))
    return pl.pallas_call(
        finish_kernel,
        out_shape=jax.ShapeDtypeStruct((rows, width), jnp.bfloat16),
        grid_spec=pltpu.PrefetchScalarGridSpec(
            num_scalar_prefetch=1,
            grid=(3 + width // WIDE,),
            in_specs=[first, first]
            + [tree] * 4
            + [pl.BlockSpec((quarter, width), lambda i, s: (jnp.minimum(i, 3) ^ s[0], 0))],
            out_specs=pl.BlockSpec((rows, WIDE), lambda i, s: (0, jnp.maximum(i - 3, 0))),
            scratch_shapes=[
                pltpu.VMEM((rows, quarter), jnp.bfloat16),
                pltpu.VMEM((width // WIDE, rows, WIDE), jnp.float32),
            ],
        ),
        compiler_params=pltpu.CompilerParams(vmem_limit_bytes=mib(FINISH_MIB)),
        cost_estimate=pl.CostEstimate(
            flops=2 * rows * width * (width + WIDE),
            bytes_accessed=6 * rows * width + 2 * width * width,
            transcendentals=0,
        ),
        name="finish",
    )(place, mixed, query, *trees, out_weight)


def swap(block, axis, mask):
    return lax.ppermute(block, axis, [(i, i ^ mask) for i in range(lax.axis_size(axis))])


def picked(flag, block):
    return jnp.where(flag, block, 0.0)


def per_device(queries, keys, values, level_weights, out_weight):
    levels, heads = level_weights.shape
    pairs = heads // 2
    inner = lax.axis_index("inner")
    outer = lax.axis_index("outer")
    x, y, core, z = inner & 3, inner >> 2, outer & 1, outer >> 1
    scale = jnp.array([1.0] + [math.sqrt(1.0 / 2 ** (l - 1)) for l in range(1, levels)], jnp.float32)
    spread = jnp.repeat((level_weights * scale[:, None]).reshape(levels, pairs, 2), SPAN, axis=2)
    table = jnp.pad(spread.transpose(1, 0, 2), ((0, 0), (0, 16 - levels), (0, 0)))
    place = x.astype(jnp.int32).reshape(1)

    queries, keys, values, out_weight = map(in_hbm, (queries, keys, values, out_weight))
    unit_keys, *sent = device_totals(place, keys, values)
    unit_keys = in_hbm(unit_keys)

    def beside(arrived, done, piece):
        done = inside(table, queries, unit_keys, values, piece, done)
        arrived, done = lax.optimization_barrier((arrived, done))
        return arrived, [in_hbm(t) for t in done]

    from_x = [swap(sent[m], "inner", m) for m in (1, 2, 3)]
    from_x, done = beside(from_x, (), 0)
    from_x = [sent[0]] + from_x
    group = from_x[0] + from_x[1] + from_x[2] + from_x[3]

    from_y = [swap(group, "inner", 4 * n) for n in (1, 2, 3)]
    from_y, done = beside(from_y, done, 1)
    from_y = [group] + from_y
    block = from_y[0] + from_y[1] + from_y[2] + from_y[3]

    other = swap(block, "outer", 1)
    other, done = beside(other, done, 2)
    both = block + other

    from_z = [swap(both, "outer", 2 * k) for k in (1, 2, 3)]
    from_z, done = beside(from_z, done, 3)

    ours = lax.dynamic_slice_in_dim(spread, 4 * x, 4, 1)[:, :, None, :]
    upper = picked(y & 1 == 1, ours[7] * from_y[1])
    upper = upper + picked(y >> 1 == 1, ours[8] * (from_y[2] + from_y[3]))
    upper = upper + picked(core == 1, ours[9] * other)
    upper = upper + picked(z & 1 == 1, ours[10] * from_z[0])
    upper = upper + picked(z >> 1 == 1, ours[11] * (from_z[1] + from_z[2]))
    to_x = []
    for m in range(4):
        near = picked((x ^ m) & 1 == 1, ours[5] * from_x[m ^ 1])
        far = picked((x ^ m) >> 1 == 1, ours[6] * (from_x[m ^ 2] + from_x[m ^ 3]))
        to_x.append(near + far + upper)
    trees = [swap(to_x[m], "inner", m) for m in (1, 2, 3)]
    trees, done = beside(trees, done, 4)
    return finish(place, *done, [to_x[0]] + trees, out_weight)


def solution(mesh):
    in_specs = (
        P(("outer", "inner"), None),
        P(("outer", "inner"), None),
        P(("outer", "inner"), None),
        P(),
        P(),
    )
    out_specs = P(("outer", "inner"), None)
    return jax.shard_map(
        per_device, mesh=mesh, in_specs=in_specs, out_specs=out_specs, check_vma=False
    )
```

```python
import functools
import math

import jax
import jax.numpy as jnp
from jax import lax
from jax.experimental import pallas as pl
from jax.experimental.pallas import tpu as pltpu
from jax.sharding import PartitionSpec as P

SPAN = 64
LANES = 128
WIDE = 256
PIECES = (2, 2, 2, 2)
TOTALS_WIDE = 512
LAST = 2
INSIDE_MIB = 32
FINISH_MIB = 40
EPS = 1e-06


def in_hbm(array):
    return pltpu.with_memory_space_constraint(array, pltpu.HBM)


def mib(count):
    return count * 1024 * 1024


def same_head(size, kind):
    row = lax.broadcasted_iota(jnp.int32, (size, size), 0) // SPAN
    col = lax.broadcasted_iota(jnp.int32, (size, size), 1) // SPAN
    return jnp.where(row == col, 1.0, 0.0).astype(kind)


def inverse_norm(block):
    total = jnp.dot(
        block * block, same_head(block.shape[1], block.dtype), preferred_element_type=jnp.float32
    )
    return lax.rsqrt(total + EPS)


def scaled(block, factor):
    return (block.astype(jnp.float32) * factor).astype(jnp.bfloat16)


def pair_state(turned, values):
    both = jnp.dot(turned, values, preferred_element_type=jnp.float32)
    lane = lax.broadcasted_iota(jnp.int32, (SPAN, LANES), 1)
    return jnp.where(lane < SPAN, both[:SPAN], both[SPAN:])


def by_head(block, low):
    zero = jnp.zeros_like(block)
    return jnp.concatenate([jnp.where(low, block, zero), jnp.where(low, zero, block)], axis=0)


def totals_kernel(where_ref, k_ref, v_ref, kt_ref, *outs):
    *outs, held = outs
    step = pl.program_id(0)
    pairs = k_ref.shape[1] // LANES
    factors = [inverse_norm(k_ref[:, at : at + WIDE]) for at in range(0, k_ref.shape[1], WIDE)]
    for group, factor in enumerate(factors):
        cut = slice(group * WIDE, (group + 1) * WIDE)
        kt_ref[cut, :] = scaled(k_ref[:, cut], factor).T
    states = []
    for pair in range(pairs):
        cut = slice(pair * LANES, (pair + 1) * LANES)
        states.append(pair_state(kt_ref[cut, :], v_ref[:, cut]))
    for pair, state in enumerate(states):
        held[step * pairs + pair] = state

    @pl.when(step == pl.num_programs(0) - 1)
    def _():
        for index, out in enumerate(outs):
            first = (where_ref[0] ^ index) * 4
            for pair in range(4):
                out[pair] = held[first + pair]


def device_totals(place, keys, values):
    rows, width = keys.shape
    step_width = TOTALS_WIDE
    steps = width // step_width
    block = pl.BlockSpec((rows, step_width), lambda i, s: (0, i))
    whole = pl.BlockSpec((4, SPAN, LANES), lambda i, s: (0, 0, 0))
    return pl.pallas_call(
        totals_kernel,
        out_shape=[pltpu.HBM((width, rows), keys.dtype)]
        + [jax.ShapeDtypeStruct((4, SPAN, LANES), jnp.float32)] * 4,
        grid_spec=pltpu.PrefetchScalarGridSpec(
            num_scalar_prefetch=1,
            grid=(steps,),
            in_specs=[block, block],
            out_specs=[pl.BlockSpec((step_width, rows), lambda i, s: (i, 0))] + [whole] * 4,
            scratch_shapes=[pltpu.VMEM((width // LANES, SPAN, LANES), jnp.float32)],
        ),
        compiler_params=pltpu.CompilerParams(vmem_limit_bytes=mib(32)),
        cost_estimate=pl.CostEstimate(
            flops=4 * rows * width * WIDE, bytes_accessed=6 * rows * width, transcendentals=0
        ),
        name="totals",
    )(place, keys, values)


def two_span_states(turned, values):
    zero = jnp.zeros((SPAN, LANES), values.dtype)
    spread = jnp.concatenate(
        [
            jnp.concatenate([values[:SPAN], zero], axis=1),
            jnp.concatenate([zero, values[SPAN:]], axis=1),
        ],
        axis=0,
    )
    both = jnp.dot(turned, spread, preferred_element_type=jnp.float32)
    lane = lax.broadcasted_iota(jnp.int32, (SPAN, LANES), 1)
    return [
        jnp.where(lane < SPAN, both[:SPAN, at : at + LANES], both[SPAN:, at : at + LANES])
        for at in (0, LANES)
    ]


def level_scale(level):
    return math.sqrt(1.0 / 2 ** max(level - 1, 0))


def blend(states, weight):
    spans = len(states)
    mix = [None] * spans
    level = states
    for bit in range(spans.bit_length() - 1):
        size = 1 << bit
        for node in range(0, len(level), 2):
            term = level[node] * weight[1 + bit]
            for c in range((node + 1) * size, (node + 2) * size):
                mix[c] = term if mix[c] is None else mix[c] + term
        level = [level[n] + level[n + 1] for n in range(0, len(level), 2)]
    return mix


def inside_kernel(start, w_ref, q_ref, kt_ref, v_ref, *refs):
    y_ref, qn_ref, seen_ref = refs[-3:]
    rows = q_ref.shape[0]
    spans = rows // SPAN
    query = q_ref[...]
    query = scaled(query, inverse_norm(query))
    qn_ref[...] = query
    lane = lax.broadcasted_iota(jnp.int32, (SPAN, LANES), 1)
    low = lane < SPAN
    seen = (lane % SPAN) <= lax.broadcasted_iota(jnp.int32, (SPAN, LANES), 0)
    pairs = [slice(at, at + LANES) for at in range(0, q_ref.shape[1], LANES)]
    first = lax.broadcasted_iota(jnp.int32, (1, LANES), 1) < SPAN
    head = (start + pl.program_id(0)) * 4
    weights = [
        [
            jnp.where(first, w_ref[level, head + 2 * pair], w_ref[level, head + 2 * pair + 1])
            * level_scale(level)
            for level in range(spans.bit_length())
        ]
        for pair in range(len(pairs))
    ]
    parts = [slice(c * SPAN, (c + 1) * SPAN) for c in range(spans)]
    states = []
    for pair, cut in enumerate(pairs):
        states.append([])
        for block in range(spans // 2):
            part = slice(block * 2 * SPAN, (block + 1) * 2 * SPAN)
            states[pair] += two_span_states(kt_ref[cut, part], v_ref[part, cut])
    for pair, cut in enumerate(pairs):
        factor = jnp.where(seen, weights[pair][0], 0.0)
        for block in range(spans // 2):
            turned = kt_ref[cut, block * 2 * SPAN : (block + 1) * 2 * SPAN]
            moved = jnp.concatenate([turned[:, SPAN:], turned[:, :SPAN]], axis=1)
            zero = jnp.zeros((SPAN, LANES), turned.dtype)
            for odd, (top, bottom) in enumerate(((turned, moved), (moved, turned))):
                part = parts[2 * block + odd]
                right = jnp.concatenate(
                    [jnp.where(low, top[:SPAN], zero), jnp.where(low, zero, bottom[SPAN:])], axis=0
                )
                scores = jnp.dot(qn_ref[part, cut], right, preferred_element_type=jnp.float32)
                seen_ref[part, cut] = (scores * factor).astype(jnp.bfloat16)
    mixes = [blend(states[pair], weights[pair]) for pair in range(len(pairs))]
    for pair, cut in enumerate(pairs):
        for c, part in enumerate(parts):
            left = seen_ref[part, cut]
            right = by_head(v_ref[part, cut], low)
            if c > 0:
                left = jnp.concatenate([left, qn_ref[part, cut]], axis=1)
                right = jnp.concatenate(
                    [right, by_head(mixes[pair][c].astype(jnp.bfloat16), low)], axis=0
                )
            y_ref[part, cut] = jnp.dot(left, right, preferred_element_type=jnp.float32).astype(
                jnp.bfloat16
            )


def inside(weights, queries, keys, values, piece, so_far):
    rows, width = queries.shape
    steps = PIECES[piece]
    start = sum(PIECES[:piece])
    block = pl.BlockSpec((rows, WIDE), lambda i: (0, start + i))
    turned = pl.BlockSpec((WIDE, rows), lambda i: (start + i, 0))
    table = pl.BlockSpec(memory_space=pltpu.SMEM)
    count = len(so_far)
    return pl.pallas_call(
        functools.partial(inside_kernel, start),
        out_shape=[pltpu.HBM((rows, width), jnp.bfloat16)] * 2,
        grid_spec=pltpu.PrefetchScalarGridSpec(
            num_scalar_prefetch=0,
            grid=(steps,),
            in_specs=[table, block, turned, block] + [pl.BlockSpec(memory_space=pl.ANY)] * count,
            out_specs=[block, block],
            scratch_shapes=[
                pltpu.VMEM((rows, WIDE), jnp.bfloat16),
            ],
        ),
        input_output_aliases={4 + n: n for n in range(count)},
        compiler_params=pltpu.CompilerParams(vmem_limit_bytes=mib(INSIDE_MIB)),
        cost_estimate=pl.CostEstimate(
            flops=16 * rows * WIDE * steps * WIDE,
            bytes_accessed=10 * rows * WIDE * steps,
            transcendentals=0,
        ),
        name="inside",
    )(weights, queries, keys, values, *so_far)


def finish_kernel(where_ref, y_ref, q_ref, *refs):
    trees = refs[:4]
    w_ref, out_ref, left, total = refs[4:]
    step = pl.program_id(0)

    @pl.when(step <= 3)
    def _():
        low = lax.broadcasted_iota(jnp.int32, (SPAN, LANES), 1) < SPAN
        blocks = []
        for slot in range(4):
            tree = trees[0][slot]
            for m in range(1, 4):
                tree = jnp.where(step == m, trees[m][slot], tree)
            tree = by_head(tree.astype(jnp.bfloat16), low)
            zero = jnp.zeros_like(tree)
            blocks.append(jnp.concatenate([tree, zero] if slot % 2 == 0 else [zero, tree], axis=1))
        for group in range(2):
            cut = slice(group * WIDE, (group + 1) * WIDE)
            mixed = y_ref[:, cut].astype(jnp.float32) + jnp.dot(
                q_ref[:, cut],
                jnp.concatenate(blocks[2 * group : 2 * group + 2], axis=0),
                preferred_element_type=jnp.float32,
            )
            left[:, cut] = mixed.astype(jnp.bfloat16)

    def product(cut):
        return jnp.dot(left[...], w_ref[:, cut], preferred_element_type=jnp.float32)

    @pl.when(step == 0)
    def _():
        for n in range(total.shape[0]):
            total[n] = product(slice(n * WIDE, (n + 1) * WIDE))

    @pl.when((step > 0) & (step < 3))
    def _():
        for n in range(total.shape[0]):
            total[n] += product(slice(n * WIDE, (n + 1) * WIDE))

    @pl.when(step >= 3)
    def _():
        each = out_ref.shape[1] // WIDE
        for k in range(each):
            n = jnp.maximum(step - 3, 0) * each + k
            cut = pl.ds(pl.multiple_of(n * WIDE, WIDE), WIDE)
            out_ref[:, k * WIDE : (k + 1) * WIDE] = (total[n] + product(cut)).astype(jnp.bfloat16)


def finish(place, mixed, query, trees, out_weight):
    rows = mixed.shape[0]
    width = out_weight.shape[0]
    quarter = width // 4
    first = pl.BlockSpec((rows, quarter), lambda i, s: (0, jnp.minimum(i, 3) ^ s[0]))
    tree = pl.BlockSpec((4, SPAN, LANES), lambda i, s: (0, 0, 0), pipeline_mode=pl.Buffered(1))
    return pl.pallas_call(
        finish_kernel,
        out_shape=jax.ShapeDtypeStruct((rows, width), jnp.bfloat16),
        grid_spec=pltpu.PrefetchScalarGridSpec(
            num_scalar_prefetch=1,
            grid=(3 + LAST,),
            in_specs=[first, first]
            + [tree] * 4
            + [pl.BlockSpec((quarter, width), lambda i, s: (jnp.minimum(i, 3) ^ s[0], 0))],
            out_specs=pl.BlockSpec((rows, width // LAST), lambda i, s: (0, jnp.maximum(i - 3, 0))),
            scratch_shapes=[
                pltpu.VMEM((rows, quarter), jnp.bfloat16),
                pltpu.VMEM((width // WIDE, rows, WIDE), jnp.float32),
            ],
        ),
        compiler_params=pltpu.CompilerParams(vmem_limit_bytes=mib(FINISH_MIB)),
        cost_estimate=pl.CostEstimate(
            flops=2 * rows * width * (width + WIDE),
            bytes_accessed=6 * rows * width + 2 * width * width,
            transcendentals=0,
        ),
        name="finish",
    )(place, mixed, query, *trees, out_weight)


def swap(block, axis, mask):
    return lax.ppermute(block, axis, [(i, i ^ mask) for i in range(lax.axis_size(axis))])


def picked(flag, block):
    return jnp.where(flag, block, 0.0)


def per_device(queries, keys, values, level_weights, out_weight):
    levels, heads = level_weights.shape
    inner = lax.axis_index("inner")
    outer = lax.axis_index("outer")
    x, y, core, z = inner & 3, inner >> 2, outer & 1, outer >> 1
    near_heads = lax.dynamic_slice_in_dim(level_weights, 8 * x, 8, 1).reshape(levels, 4, 2, 1)
    ours = jnp.broadcast_to(near_heads, (levels, 4, 2, SPAN)).reshape(levels, 4, 1, LANES)
    ours = [ours[level] * level_scale(level) for level in range(levels)]
    place = x.astype(jnp.int32).reshape(1)

    queries, keys, values, out_weight = map(in_hbm, (queries, keys, values, out_weight))
    turned_keys, *sent = device_totals(place, keys, values)
    turned_keys = in_hbm(turned_keys)

    def beside(arrived, done, piece):
        done = inside(level_weights, queries, turned_keys, values, piece, done)
        arrived, done = lax.optimization_barrier((arrived, done))
        return arrived, [in_hbm(t) for t in done]

    from_x = [swap(sent[m], "inner", m) for m in (1, 2, 3)]
    from_x, done = beside(from_x, (), 0)
    from_x = [sent[0]] + from_x
    group = from_x[0] + from_x[1] + from_x[2] + from_x[3]

    from_y = [swap(group, "inner", 4 * n) for n in (1, 2, 3)]
    from_y, done = beside(from_y, done, 1)
    from_y = [group] + from_y
    block = from_y[0] + from_y[1] + from_y[2] + from_y[3]

    other = swap(block, "outer", 1)
    both = block + other

    from_z = [swap(both, "outer", 2 * k) for k in (1, 2, 3)]
    from_z, done = beside(from_z, done, 2)

    upper = picked(y & 1 == 1, ours[7] * from_y[1])
    upper = upper + picked(y >> 1 == 1, ours[8] * (from_y[2] + from_y[3]))
    upper = upper + picked(core == 1, ours[9] * other)
    upper = upper + picked(z & 1 == 1, ours[10] * from_z[0])
    upper = upper + picked(z >> 1 == 1, ours[11] * (from_z[1] + from_z[2]))
    to_x = []
    for m in range(4):
        near = picked((x ^ m) & 1 == 1, ours[5] * from_x[m ^ 1])
        far = picked((x ^ m) >> 1 == 1, ours[6] * (from_x[m ^ 2] + from_x[m ^ 3]))
        to_x.append(near + far + upper)
    trees = [swap(to_x[m], "inner", m) for m in (1, 2, 3)]
    trees, done = beside(trees, done, 3)
    return finish(place, *done, [to_x[0]] + trees, out_weight)


def solution(mesh):
    in_specs = (
        P(("outer", "inner"), None),
        P(("outer", "inner"), None),
        P(("outer", "inner"), None),
        P(),
        P(),
    )
    out_specs = P(("outer", "inner"), None)
    return jax.shard_map(
        per_device, mesh=mesh, in_specs=in_specs, out_specs=out_specs, check_vma=False
    )
```

```python
import functools
import math

import jax
import jax.numpy as jnp
from jax import lax
from jax.experimental import pallas as pl
from jax.experimental.pallas import tpu as pltpu
from jax.sharding import PartitionSpec as P


SPAN = 64
LANES = 128
WIDE = 256
TOTALS_WIDE = 512
LAST = 2
INSIDE_MIB = 32
FINISH_MIB = 40
EPS = 1e-06


def in_hbm(array):
    return pltpu.with_memory_space_constraint(array, pltpu.HBM)


def mib(count):
    return count * 1024 * 1024


def same_head(size, kind):
    row = lax.broadcasted_iota(jnp.int32, (size, size), 0) // SPAN
    col = lax.broadcasted_iota(jnp.int32, (size, size), 1) // SPAN
    return jnp.where(row == col, 1.0, 0.0).astype(kind)


def inverse_norm(block):
    total = jnp.dot(
        block * block, same_head(block.shape[1], block.dtype), preferred_element_type=jnp.float32
    )
    return lax.rsqrt(total + EPS)


def scaled(block, factor):
    return (block.astype(jnp.float32) * factor).astype(jnp.bfloat16)


def pair_state(turned, values):
    both = jnp.dot(turned, values, preferred_element_type=jnp.float32)
    lane = lax.broadcasted_iota(jnp.int32, (SPAN, LANES), 1)
    return jnp.where(lane < SPAN, both[:SPAN], both[SPAN:])


def by_head(block, low):
    zero = jnp.zeros_like(block)
    return jnp.concatenate([jnp.where(low, block, zero), jnp.where(low, zero, block)], axis=0)


def totals_kernel(where_ref, k_hbm, v_hbm, kt_hbm, *refs):
    outs = refs[:4]
    k_buf, v_buf, kt_buf, held, k_sem, v_sem, kt_sem = refs[4:]
    groups = k_buf.shape[0]
    each = TOTALS_WIDE // WIDE

    def load(hbm, buf, sem, group):
        return pltpu.make_async_copy(
            hbm.at[:, group * WIDE : (group + 1) * WIDE], buf.at[group], sem.at[group]
        )

    keys = [load(k_hbm, k_buf, k_sem, group) for group in range(groups)]
    values = [load(v_hbm, v_buf, v_sem, group) for group in range(groups)]
    stores = [
        pltpu.make_async_copy(
            kt_buf.at[group], kt_hbm.at[group * WIDE : (group + 1) * WIDE, :], kt_sem.at[group]
        )
        for group in range(groups)
    ]
    turns = [range(at, at + each) for at in range(0, groups, each)]

    def fetch(turn):
        for copies in (keys, values):
            for group in turns[turn]:
                copies[group].start()

    fetch(0)
    for turn, members in enumerate(turns):
        if turn + 1 < len(turns):
            fetch(turn + 1)
        factors = []
        for group in members:
            keys[group].wait()
            if turn > 0:
                values[group].wait()
        for group in members:
            factors.append(inverse_norm(k_buf[group]))
        for group, factor in zip(members, factors):
            kt_buf[group] = scaled(k_buf[group], factor).T
        if turn == 0:
            for group in members:
                values[group].wait()
        for group in members:
            for pair in range(WIDE // LANES):
                cut = slice(pair * LANES, (pair + 1) * LANES)
                held[group * (WIDE // LANES) + pair] = pair_state(
                    kt_buf[group, cut, :], v_buf[group, :, cut]
                )
        for group in members:
            stores[group].start()
    for index, out in enumerate(outs):
        first = (where_ref[0] ^ index) * 4
        for pair in range(4):
            out[pair] = held[first + pair]
    for copy in stores:
        copy.wait()


def device_totals(place, keys, values):
    rows, width = keys.shape
    groups = width // WIDE
    here = pl.BlockSpec(memory_space=pl.ANY)
    near = pl.BlockSpec(memory_space=pltpu.VMEM)
    return pl.pallas_call(
        totals_kernel,
        out_shape=[pltpu.HBM((width, rows), keys.dtype)]
        + [jax.ShapeDtypeStruct((4, SPAN, LANES), jnp.float32)] * 4,
        in_specs=[pl.BlockSpec(memory_space=pltpu.SMEM), here, here],
        out_specs=[here] + [near] * 4,
        scratch_shapes=[
            pltpu.VMEM((groups, rows, WIDE), jnp.bfloat16),
            pltpu.VMEM((groups, rows, WIDE), jnp.bfloat16),
            pltpu.VMEM((groups, WIDE, rows), jnp.bfloat16),
            pltpu.VMEM((width // LANES, SPAN, LANES), jnp.float32),
            pltpu.SemaphoreType.DMA((groups,)),
            pltpu.SemaphoreType.DMA((groups,)),
            pltpu.SemaphoreType.DMA((groups,)),
        ],
        compiler_params=pltpu.CompilerParams(vmem_limit_bytes=mib(40)),
        cost_estimate=pl.CostEstimate(
            flops=4 * rows * width * WIDE, bytes_accessed=6 * rows * width, transcendentals=0
        ),
        name="totals",
    )(place, keys, values)


def two_span_states(turned, values):
    zero = jnp.zeros((SPAN, LANES), values.dtype)
    spread = jnp.concatenate(
        [
            jnp.concatenate([values[:SPAN], zero], axis=1),
            jnp.concatenate([zero, values[SPAN:]], axis=1),
        ],
        axis=0,
    )
    both = jnp.dot(turned, spread, preferred_element_type=jnp.float32)
    lane = lax.broadcasted_iota(jnp.int32, (SPAN, LANES), 1)
    return [
        jnp.where(lane < SPAN, both[:SPAN, at : at + LANES], both[SPAN:, at : at + LANES])
        for at in (0, LANES)
    ]


def level_scale(level):
    return math.sqrt(1.0 / 2 ** max(level - 1, 0))


def blend(states, weight):
    spans = len(states)
    mix = [None] * spans
    level = states
    for bit in range(spans.bit_length() - 1):
        size = 1 << bit
        for node in range(0, len(level), 2):
            term = level[node] * weight[1 + bit]
            for c in range((node + 1) * size, (node + 2) * size):
                mix[c] = term if mix[c] is None else mix[c] + term
        level = [level[n] + level[n + 1] for n in range(0, len(level), 2)]
    return mix


def inside_kernel(slice_of, has_tree, where_ref, w_ref, q_ref, kt_ref, v_ref, *refs):
    y_ref, qn_ref, seen_ref = refs[-3:]
    rows = q_ref.shape[0]
    spans = rows // SPAN
    query = q_ref[...]
    query = scaled(query, inverse_norm(query))
    qn_ref[...] = query
    lane = lax.broadcasted_iota(jnp.int32, (SPAN, LANES), 1)
    low = lane < SPAN
    seen = (lane % SPAN) <= lax.broadcasted_iota(jnp.int32, (SPAN, LANES), 0)
    pairs = [slice(at, at + LANES) for at in range(0, q_ref.shape[1], LANES)]
    first = lax.broadcasted_iota(jnp.int32, (1, LANES), 1) < SPAN
    head = ((where_ref[0] ^ slice_of) * 2 + pl.program_id(0)) * 4
    weights = [
        [
            jnp.where(first, w_ref[level, head + 2 * pair], w_ref[level, head + 2 * pair + 1])
            * level_scale(level)
            for level in range(spans.bit_length())
        ]
        for pair in range(len(pairs))
    ]
    parts = [slice(c * SPAN, (c + 1) * SPAN) for c in range(spans)]
    states = []
    for pair, cut in enumerate(pairs):
        states.append([])
        for block in range(spans // 2):
            part = slice(block * 2 * SPAN, (block + 1) * 2 * SPAN)
            states[pair] += two_span_states(kt_ref[cut, part], v_ref[part, cut])
    for pair, cut in enumerate(pairs):
        factor = jnp.where(seen, weights[pair][0], 0.0)
        for block in range(spans // 2):
            turned = kt_ref[cut, block * 2 * SPAN : (block + 1) * 2 * SPAN]
            moved = jnp.concatenate([turned[:, SPAN:], turned[:, :SPAN]], axis=1)
            zero = jnp.zeros((SPAN, LANES), turned.dtype)
            for odd, (top, bottom) in enumerate(((turned, moved), (moved, turned))):
                part = parts[2 * block + odd]
                right = jnp.concatenate(
                    [jnp.where(low, top[:SPAN], zero), jnp.where(low, zero, bottom[SPAN:])], axis=0
                )
                scores = jnp.dot(qn_ref[part, cut], right, preferred_element_type=jnp.float32)
                seen_ref[part, cut] = (scores * factor).astype(jnp.bfloat16)
    mixes = [blend(states[pair], weights[pair]) for pair in range(len(pairs))]
    if has_tree:
        for pair, mix in enumerate(mixes):
            tree = refs[0][pair]
            mixes[pair] = [tree if local is None else local + tree for local in mix]
    for pair, cut in enumerate(pairs):
        for c, part in enumerate(parts):
            left = seen_ref[part, cut]
            right = by_head(v_ref[part, cut], low)
            if mixes[pair][c] is not None:
                left = jnp.concatenate([left, qn_ref[part, cut]], axis=1)
                right = jnp.concatenate(
                    [right, by_head(mixes[pair][c].astype(jnp.bfloat16), low)], axis=0
                )
            y_ref[part, cut] = jnp.dot(left, right, preferred_element_type=jnp.float32).astype(
                jnp.bfloat16
            )


def inside(place, weights, queries, keys, values, slice_of, so_far, trees=()):
    rows, width = queries.shape
    steps = width // WIDE // 4
    block = pl.BlockSpec((rows, WIDE), lambda i, s: (0, (s[0] ^ slice_of) * steps + i))
    turned = pl.BlockSpec((WIDE, rows), lambda i, s: ((s[0] ^ slice_of) * steps + i, 0))
    table = pl.BlockSpec(memory_space=pltpu.SMEM)
    tree = pl.BlockSpec((2, SPAN, LANES), lambda i, s: (i, 0, 0))
    count = len(so_far)
    return pl.pallas_call(
        functools.partial(inside_kernel, slice_of, len(trees) > 0),
        out_shape=[pltpu.HBM((rows, width), jnp.bfloat16)] * 2,
        grid_spec=pltpu.PrefetchScalarGridSpec(
            num_scalar_prefetch=1,
            grid=(steps,),
            in_specs=[table, block, turned, block]
            + [tree] * len(trees)
            + [pl.BlockSpec(memory_space=pl.ANY)] * count,
            out_specs=[block, block],
            scratch_shapes=[pltpu.VMEM((rows, WIDE), jnp.bfloat16)],
        ),
        input_output_aliases={5 + len(trees) + n: n for n in range(count)},
        compiler_params=pltpu.CompilerParams(vmem_limit_bytes=mib(INSIDE_MIB)),
        cost_estimate=pl.CostEstimate(
            flops=16 * rows * WIDE * steps * WIDE,
            bytes_accessed=10 * rows * WIDE * steps,
            transcendentals=0,
        ),
        name="inside",
    )(place, weights, queries, keys, values, *trees, *so_far)


def finish_kernel(where_ref, y_ref, *refs):
    trees = refs[:3]
    q_hbm, w_ref, out_ref, left, total, q_buf, q_sem = refs[3:]
    step = pl.program_id(0)
    quarter = left.shape[1]

    def fetch(part):
        home = pl.multiple_of((where_ref[0] ^ part) * quarter, quarter)
        return pltpu.make_async_copy(
            q_hbm.at[:, pl.ds(home, quarter)], q_buf.at[part % 2], q_sem.at[part % 2]
        )

    @pl.when(step < 3)
    def _():
        fetch(step + 1).start()

    @pl.when((step > 0) & (step <= 3))
    def _():
        low = lax.broadcasted_iota(jnp.int32, (SPAN, LANES), 1) < SPAN
        blocks = []
        for slot in range(4):
            tree = trees[0][slot]
            for m in range(2, 4):
                tree = jnp.where(step == m, trees[m - 1][slot], tree)
            tree = by_head(tree.astype(jnp.bfloat16), low)
            zero = jnp.zeros_like(tree)
            blocks.append(jnp.concatenate([tree, zero] if slot % 2 == 0 else [zero, tree], axis=1))
        fetch(step).wait()
        for group in range(2):
            cut = slice(group * WIDE, (group + 1) * WIDE)
            mixed = y_ref[:, cut].astype(jnp.float32) + jnp.dot(
                q_buf[step % 2, :, cut],
                jnp.concatenate(blocks[2 * group : 2 * group + 2], axis=0),
                preferred_element_type=jnp.float32,
            )
            left[:, cut] = mixed.astype(jnp.bfloat16)

    def product(rows, cut):
        return jnp.dot(rows[...], w_ref[:, cut], preferred_element_type=jnp.float32)

    @pl.when(step == 0)
    def _():
        for n in range(total.shape[0]):
            total[n] = product(y_ref, slice(n * WIDE, (n + 1) * WIDE))

    @pl.when((step > 0) & (step < 3))
    def _():
        for n in range(total.shape[0]):
            total[n] += product(left, slice(n * WIDE, (n + 1) * WIDE))

    @pl.when(step >= 3)
    def _():
        each = out_ref.shape[1] // WIDE
        for k in range(each):
            n = jnp.maximum(step - 3, 0) * each + k
            cut = pl.ds(pl.multiple_of(n * WIDE, WIDE), WIDE)
            out_ref[:, k * WIDE : (k + 1) * WIDE] = (total[n] + product(left, cut)).astype(
                jnp.bfloat16
            )


def finish(place, mixed, query, trees, out_weight):
    rows = mixed.shape[0]
    width = out_weight.shape[0]
    quarter = width // 4
    first = pl.BlockSpec((rows, quarter), lambda i, s: (0, jnp.minimum(i, 3) ^ s[0]))
    tree = pl.BlockSpec((4, SPAN, LANES), lambda i, s: (0, 0, 0), pipeline_mode=pl.Buffered(1))
    return pl.pallas_call(
        finish_kernel,
        out_shape=jax.ShapeDtypeStruct((rows, width), jnp.bfloat16),
        grid_spec=pltpu.PrefetchScalarGridSpec(
            num_scalar_prefetch=1,
            grid=(3 + LAST,),
            in_specs=[first]
            + [tree] * 3
            + [pl.BlockSpec(memory_space=pl.ANY)]
            + [pl.BlockSpec((quarter, width), lambda i, s: (jnp.minimum(i, 3) ^ s[0], 0))],
            out_specs=pl.BlockSpec((rows, width // LAST), lambda i, s: (0, jnp.maximum(i - 3, 0))),
            scratch_shapes=[
                pltpu.VMEM((rows, quarter), jnp.bfloat16),
                pltpu.VMEM((width // WIDE, rows, WIDE), jnp.float32),
                pltpu.VMEM((2, rows, quarter), jnp.bfloat16),
                pltpu.SemaphoreType.DMA((2,)),
            ],
        ),
        compiler_params=pltpu.CompilerParams(vmem_limit_bytes=mib(FINISH_MIB)),
        cost_estimate=pl.CostEstimate(
            flops=2 * rows * width * (width + WIDE),
            bytes_accessed=6 * rows * width + 2 * width * width,
            transcendentals=0,
        ),
        name="finish",
    )(place, mixed, *trees, query, out_weight)


def swap(block, axis, mask):
    return lax.ppermute(block, axis, [(i, i ^ mask) for i in range(lax.axis_size(axis))])


def swap_three(block_of, axis, unit):
    arrived = []
    for m in (1, 2, 3):
        arrived.append(swap(block_of(m), axis, m * unit))
    return arrived


def picked(flag, block):
    return jnp.where(flag, block, 0.0)


def per_device(queries, keys, values, level_weights, out_weight):
    levels, _ = level_weights.shape
    inner = lax.axis_index("inner")
    outer = lax.axis_index("outer")
    x, y, core, z = inner & 3, inner >> 2, outer & 1, outer >> 1
    near_heads = lax.dynamic_slice_in_dim(level_weights, 8 * x, 8, 1).reshape(levels, 4, 2, 1)
    ours = jnp.broadcast_to(near_heads, (levels, 4, 2, SPAN)).reshape(levels, 4, 1, LANES)
    ours = [ours[level] * level_scale(level) for level in range(levels)]
    place = x.astype(jnp.int32).reshape(1)

    queries, keys, values, out_weight = map(in_hbm, (queries, keys, values, out_weight))
    turned_keys, *sent = device_totals(place, keys, values)
    turned_keys = in_hbm(turned_keys)

    def beside(arrived, done, slice_of, tree=()):
        done = inside(place, level_weights, queries, turned_keys, values, slice_of, done, tree)
        arrived, done = lax.optimization_barrier((arrived, done))
        return arrived, [in_hbm(t) for t in done]

    from_x = swap_three(lambda m: sent[m], "inner", 1)
    from_x, done = beside(from_x, (), 1)
    from_x = [sent[0]] + from_x
    group = from_x[0] + from_x[1] + from_x[2] + from_x[3]

    from_y = swap_three(lambda n: group, "inner", 4)
    from_y, done = beside(from_y, done, 2)
    from_y = [group] + from_y
    block = from_y[0] + from_y[1] + from_y[2] + from_y[3]

    other = swap(block, "outer", 1)
    both = block + other

    from_z = swap_three(lambda n: both, "outer", 2)
    from_z, done = beside(from_z, done, 3)

    upper = picked(y & 1 == 1, ours[7] * from_y[1])
    upper = upper + picked(y >> 1 == 1, ours[8] * (from_y[2] + from_y[3]))
    upper = upper + picked(core == 1, ours[9] * other)
    upper = upper + picked(z & 1 == 1, ours[10] * from_z[0])
    upper = upper + picked(z >> 1 == 1, ours[11] * (from_z[1] + from_z[2]))
    to_x = []
    for m in range(4):
        near = picked((x ^ m) & 1 == 1, ours[5] * from_x[m ^ 1])
        far = picked((x ^ m) >> 1 == 1, ours[6] * (from_x[m ^ 2] + from_x[m ^ 3]))
        to_x.append(near + far + upper)
    trees = swap_three(lambda m: to_x[m], "inner", 1)
    trees, done = beside(trees, done, 0, (to_x[0],))
    return finish(place, *done, trees, out_weight)


def solution(mesh):
    in_specs = (
        P(("outer", "inner"), None),
        P(("outer", "inner"), None),
        P(("outer", "inner"), None),
        P(),
        P(),
    )
    out_specs = P(("outer", "inner"), None)
    return jax.shard_map(per_device, mesh=mesh, in_specs=in_specs, out_specs=out_specs, check_vma=False)
```

```python
import functools
import math

import jax
import jax.numpy as jnp
from jax import lax
from jax.experimental import pallas as pl
from jax.experimental.pallas import tpu as pltpu
from jax.sharding import PartitionSpec as P


SPAN = 64
LANES = 128
WIDE = 256
TURNS = (2, 3, 3)
LAST = 2
INSIDE_MIB = 32
FINISH_MIB = 40
EPS = 1e-06


def in_hbm(array):
    return pltpu.with_memory_space_constraint(array, pltpu.HBM)


def mib(count):
    return count * 1024 * 1024


def same_head(size, kind):
    row = lax.broadcasted_iota(jnp.int32, (size, size), 0) // SPAN
    col = lax.broadcasted_iota(jnp.int32, (size, size), 1) // SPAN
    return jnp.where(row == col, 1.0, 0.0).astype(kind)


def inverse_norm(block):
    total = jnp.dot(
        block * block, same_head(block.shape[1], block.dtype), preferred_element_type=jnp.float32
    )
    return lax.rsqrt(total + EPS)


def scaled(block, factor):
    return (block.astype(jnp.float32) * factor).astype(jnp.bfloat16)


def pair_state(turned, values):
    both = jnp.dot(turned, values, preferred_element_type=jnp.float32)
    lane = lax.broadcasted_iota(jnp.int32, (SPAN, LANES), 1)
    return jnp.where(lane < SPAN, both[:SPAN], both[SPAN:])


def by_head(block, low):
    zero = jnp.zeros_like(block)
    return jnp.concatenate([jnp.where(low, block, zero), jnp.where(low, zero, block)], axis=0)


def totals_kernel(where_ref, k_hbm, v_hbm, kt_hbm, *refs):
    outs = refs[:4]
    k_buf, v_buf, kt_buf, held, k_sem, v_sem, kt_sem = refs[4:]
    groups = k_buf.shape[0]

    def load(hbm, buf, sem, group):
        return pltpu.make_async_copy(
            hbm.at[:, group * WIDE : (group + 1) * WIDE], buf.at[group], sem.at[group]
        )

    keys = [load(k_hbm, k_buf, k_sem, group) for group in range(groups)]
    values = [load(v_hbm, v_buf, v_sem, group) for group in range(groups)]
    stores = [
        pltpu.make_async_copy(
            kt_buf.at[group], kt_hbm.at[group * WIDE : (group + 1) * WIDE, :], kt_sem.at[group]
        )
        for group in range(groups)
    ]
    turns = [range(sum(TURNS[:n]), sum(TURNS[: n + 1])) for n in range(len(TURNS))]

    def fetch(turn):
        for copies in (keys, values):
            for group in turns[turn]:
                copies[group].start()

    fetch(0)
    for turn, members in enumerate(turns):
        if turn + 1 < len(turns):
            fetch(turn + 1)
        factors = []
        for group in members:
            keys[group].wait()
            if turn > 0:
                values[group].wait()
        for group in members:
            factors.append(inverse_norm(k_buf[group]))
        for group, factor in zip(members, factors):
            kt_buf[group] = scaled(k_buf[group], factor).T
        if turn == 0:
            for group in members:
                values[group].wait()
        for group in members:
            for pair in range(WIDE // LANES):
                cut = slice(pair * LANES, (pair + 1) * LANES)
                held[group * (WIDE // LANES) + pair] = pair_state(
                    kt_buf[group, cut, :], v_buf[group, :, cut]
                )
        for group in members:
            stores[group].start()
    for index, out in enumerate(outs):
        first = (where_ref[0] ^ index) * 4
        for pair in range(4):
            out[pair] = held[first + pair]
    for copy in stores:
        copy.wait()


def device_totals(place, keys, values):
    rows, width = keys.shape
    groups = width // WIDE
    here = pl.BlockSpec(memory_space=pl.ANY)
    near = pl.BlockSpec(memory_space=pltpu.VMEM)
    return pl.pallas_call(
        totals_kernel,
        out_shape=[pltpu.HBM((width, rows), keys.dtype)]
        + [jax.ShapeDtypeStruct((4, SPAN, LANES), jnp.float32)] * 4,
        in_specs=[pl.BlockSpec(memory_space=pltpu.SMEM), here, here],
        out_specs=[here] + [near] * 4,
        scratch_shapes=[
            pltpu.VMEM((groups, rows, WIDE), jnp.bfloat16),
            pltpu.VMEM((groups, rows, WIDE), jnp.bfloat16),
            pltpu.VMEM((groups, WIDE, rows), jnp.bfloat16),
            pltpu.VMEM((width // LANES, SPAN, LANES), jnp.float32),
            pltpu.SemaphoreType.DMA((groups,)),
            pltpu.SemaphoreType.DMA((groups,)),
            pltpu.SemaphoreType.DMA((groups,)),
        ],
        compiler_params=pltpu.CompilerParams(vmem_limit_bytes=mib(40)),
        cost_estimate=pl.CostEstimate(
            flops=4 * rows * width * WIDE, bytes_accessed=6 * rows * width, transcendentals=0
        ),
        name="totals",
    )(place, keys, values)


def two_span_states(turned, values):
    zero = jnp.zeros((SPAN, LANES), values.dtype)
    spread = jnp.concatenate(
        [
            jnp.concatenate([values[:SPAN], zero], axis=1),
            jnp.concatenate([zero, values[SPAN:]], axis=1),
        ],
        axis=0,
    )
    both = jnp.dot(turned, spread, preferred_element_type=jnp.float32)
    lane = lax.broadcasted_iota(jnp.int32, (SPAN, LANES), 1)
    return [
        jnp.where(lane < SPAN, both[:SPAN, at : at + LANES], both[SPAN:, at : at + LANES])
        for at in (0, LANES)
    ]


def level_scale(level):
    return math.sqrt(1.0 / 2 ** max(level - 1, 0))


def blend(states, weight):
    spans = len(states)
    mix = [None] * spans
    level = states
    for bit in range(spans.bit_length() - 1):
        size = 1 << bit
        for node in range(0, len(level), 2):
            term = level[node] * weight[1 + bit]
            for c in range((node + 1) * size, (node + 2) * size):
                mix[c] = term if mix[c] is None else mix[c] + term
        level = [level[n] + level[n + 1] for n in range(0, len(level), 2)]
    return mix


def inside_kernel(slice_of, has_tree, where_ref, w_ref, q_ref, kt_ref, v_ref, *refs):
    y_ref, qn_ref, seen_ref = refs[-3:]
    rows = q_ref.shape[0]
    spans = rows // SPAN
    query = q_ref[...]
    query = scaled(query, inverse_norm(query))
    qn_ref[...] = query
    lane = lax.broadcasted_iota(jnp.int32, (SPAN, LANES), 1)
    low = lane < SPAN
    seen = (lane % SPAN) <= lax.broadcasted_iota(jnp.int32, (SPAN, LANES), 0)
    pairs = [slice(at, at + LANES) for at in range(0, q_ref.shape[1], LANES)]
    first = lax.broadcasted_iota(jnp.int32, (1, LANES), 1) < SPAN
    head = ((where_ref[0] ^ slice_of) * 2 + pl.program_id(0)) * 4
    weights = [
        [
            jnp.where(first, w_ref[level, head + 2 * pair], w_ref[level, head + 2 * pair + 1])
            * level_scale(level)
            for level in range(spans.bit_length())
        ]
        for pair in range(len(pairs))
    ]
    parts = [slice(c * SPAN, (c + 1) * SPAN) for c in range(spans)]
    states = []
    for pair, cut in enumerate(pairs):
        states.append([])
        for block in range(spans // 2):
            part = slice(block * 2 * SPAN, (block + 1) * 2 * SPAN)
            states[pair] += two_span_states(kt_ref[cut, part], v_ref[part, cut])
    for pair, cut in enumerate(pairs):
        factor = jnp.where(seen, weights[pair][0], 0.0)
        for block in range(spans // 2):
            turned = kt_ref[cut, block * 2 * SPAN : (block + 1) * 2 * SPAN]
            moved = jnp.concatenate([turned[:, SPAN:], turned[:, :SPAN]], axis=1)
            zero = jnp.zeros((SPAN, LANES), turned.dtype)
            for odd, (top, bottom) in enumerate(((turned, moved), (moved, turned))):
                part = parts[2 * block + odd]
                right = jnp.concatenate(
                    [jnp.where(low, top[:SPAN], zero), jnp.where(low, zero, bottom[SPAN:])], axis=0
                )
                scores = jnp.dot(qn_ref[part, cut], right, preferred_element_type=jnp.float32)
                seen_ref[part, cut] = (scores * factor).astype(jnp.bfloat16)
    mixes = [blend(states[pair], weights[pair]) for pair in range(len(pairs))]
    if has_tree:
        for pair, mix in enumerate(mixes):
            tree = refs[0][pair]
            mixes[pair] = [tree if local is None else local + tree for local in mix]
    for pair, cut in enumerate(pairs):
        for c, part in enumerate(parts):
            left = seen_ref[part, cut]
            right = by_head(v_ref[part, cut], low)
            if mixes[pair][c] is not None:
                left = jnp.concatenate([left, qn_ref[part, cut]], axis=1)
                right = jnp.concatenate(
                    [right, by_head(mixes[pair][c].astype(jnp.bfloat16), low)], axis=0
                )
            y_ref[part, cut] = jnp.dot(left, right, preferred_element_type=jnp.float32).astype(
                jnp.bfloat16
            )


def inside(place, weights, queries, keys, values, slice_of, so_far, trees=()):
    rows, width = queries.shape
    steps = width // WIDE // 4
    block = pl.BlockSpec((rows, WIDE), lambda i, s: (0, (s[0] ^ slice_of) * steps + i))
    turned = pl.BlockSpec((WIDE, rows), lambda i, s: ((s[0] ^ slice_of) * steps + i, 0))
    table = pl.BlockSpec(memory_space=pltpu.SMEM)
    tree = pl.BlockSpec((2, SPAN, LANES), lambda i, s: (i, 0, 0))
    count = len(so_far)
    return pl.pallas_call(
        functools.partial(inside_kernel, slice_of, len(trees) > 0),
        out_shape=[pltpu.HBM((rows, width), jnp.bfloat16)] * 2,
        grid_spec=pltpu.PrefetchScalarGridSpec(
            num_scalar_prefetch=1,
            grid=(steps,),
            in_specs=[table, block, turned, block]
            + [tree] * len(trees)
            + [pl.BlockSpec(memory_space=pl.ANY)] * count,
            out_specs=[block, block],
            scratch_shapes=[pltpu.VMEM((rows, WIDE), jnp.bfloat16)],
        ),
        input_output_aliases={5 + len(trees) + n: n for n in range(count)},
        compiler_params=pltpu.CompilerParams(vmem_limit_bytes=mib(INSIDE_MIB)),
        cost_estimate=pl.CostEstimate(
            flops=16 * rows * WIDE * steps * WIDE,
            bytes_accessed=10 * rows * WIDE * steps,
            transcendentals=0,
        ),
        name="inside",
    )(place, weights, queries, keys, values, *trees, *so_far)


def finish_kernel(where_ref, y_ref, *refs):
    trees = refs[:3]
    q_hbm, w_ref, out_ref, left, total, q_buf, q_sem = refs[3:]
    step = pl.program_id(0)
    quarter = left.shape[1]

    def fetch(part):
        home = pl.multiple_of((where_ref[0] ^ part) * quarter, quarter)
        return pltpu.make_async_copy(
            q_hbm.at[:, pl.ds(home, quarter)], q_buf.at[part % 2], q_sem.at[part % 2]
        )

    @pl.when(step < 3)
    def _():
        fetch(step + 1).start()

    @pl.when((step > 0) & (step <= 3))
    def _():
        low = lax.broadcasted_iota(jnp.int32, (SPAN, LANES), 1) < SPAN
        blocks = []
        for slot in range(4):
            tree = trees[0][slot]
            for m in range(2, 4):
                tree = jnp.where(step == m, trees[m - 1][slot], tree)
            tree = by_head(tree.astype(jnp.bfloat16), low)
            zero = jnp.zeros_like(tree)
            blocks.append(jnp.concatenate([tree, zero] if slot % 2 == 0 else [zero, tree], axis=1))
        fetch(step).wait()
        for group in range(2):
            cut = slice(group * WIDE, (group + 1) * WIDE)
            mixed = y_ref[:, cut].astype(jnp.float32) + jnp.dot(
                q_buf[step % 2, :, cut],
                jnp.concatenate(blocks[2 * group : 2 * group + 2], axis=0),
                preferred_element_type=jnp.float32,
            )
            left[:, cut] = mixed.astype(jnp.bfloat16)

    def product(rows, cut):
        return jnp.dot(rows[...], w_ref[:, cut], preferred_element_type=jnp.float32)

    @pl.when(step == 0)
    def _():
        for n in range(total.shape[0]):
            total[n] = product(y_ref, slice(n * WIDE, (n + 1) * WIDE))

    @pl.when((step > 0) & (step < 3))
    def _():
        for n in range(total.shape[0]):
            total[n] += product(left, slice(n * WIDE, (n + 1) * WIDE))

    @pl.when(step >= 3)
    def _():
        each = out_ref.shape[1] // WIDE
        for k in range(each):
            n = jnp.maximum(step - 3, 0) * each + k
            cut = pl.ds(pl.multiple_of(n * WIDE, WIDE), WIDE)
            out_ref[:, k * WIDE : (k + 1) * WIDE] = (total[n] + product(left, cut)).astype(
                jnp.bfloat16
            )


def finish(place, mixed, query, trees, out_weight):
    rows = mixed.shape[0]
    width = out_weight.shape[0]
    quarter = width // 4
    first = pl.BlockSpec((rows, quarter), lambda i, s: (0, jnp.minimum(i, 3) ^ s[0]))
    tree = pl.BlockSpec((4, SPAN, LANES), lambda i, s: (0, 0, 0), pipeline_mode=pl.Buffered(1))
    return pl.pallas_call(
        finish_kernel,
        out_shape=jax.ShapeDtypeStruct((rows, width), jnp.bfloat16),
        grid_spec=pltpu.PrefetchScalarGridSpec(
            num_scalar_prefetch=1,
            grid=(3 + LAST,),
            in_specs=[first]
            + [tree] * 3
            + [pl.BlockSpec(memory_space=pl.ANY)]
            + [pl.BlockSpec((quarter, width), lambda i, s: (jnp.minimum(i, 3) ^ s[0], 0))],
            out_specs=pl.BlockSpec((rows, width // LAST), lambda i, s: (0, jnp.maximum(i - 3, 0))),
            scratch_shapes=[
                pltpu.VMEM((rows, quarter), jnp.bfloat16),
                pltpu.VMEM((width // WIDE, rows, WIDE), jnp.float32),
                pltpu.VMEM((2, rows, quarter), jnp.bfloat16),
                pltpu.SemaphoreType.DMA((2,)),
            ],
        ),
        compiler_params=pltpu.CompilerParams(vmem_limit_bytes=mib(FINISH_MIB)),
        cost_estimate=pl.CostEstimate(
            flops=2 * rows * width * (width + WIDE),
            bytes_accessed=6 * rows * width + 2 * width * width,
            transcendentals=0,
        ),
        name="finish",
    )(place, mixed, *trees, query, out_weight)


def swap(block, axis, mask):
    return lax.ppermute(block, axis, [(i, i ^ mask) for i in range(lax.axis_size(axis))])


def swap_three(block_of, axis, unit):
    arrived = []
    for m in (1, 2, 3):
        arrived.append(swap(block_of(m), axis, m * unit))
    return arrived


def picked(flag, block):
    return jnp.where(flag, block, 0.0)


def per_device(queries, keys, values, level_weights, out_weight):
    levels, _ = level_weights.shape
    inner = lax.axis_index("inner")
    outer = lax.axis_index("outer")
    x, y, core, z = inner & 3, inner >> 2, outer & 1, outer >> 1
    near_heads = lax.dynamic_slice_in_dim(level_weights, 8 * x, 8, 1).reshape(levels, 4, 2, 1)
    ours = jnp.broadcast_to(near_heads, (levels, 4, 2, SPAN)).reshape(levels, 4, 1, LANES)
    ours = [ours[level] * level_scale(level) for level in range(levels)]
    place = x.astype(jnp.int32).reshape(1)

    queries, keys, values, out_weight = map(in_hbm, (queries, keys, values, out_weight))
    turned_keys, *sent = device_totals(place, keys, values)
    turned_keys = in_hbm(turned_keys)

    def beside(arrived, done, slice_of, tree=()):
        done = inside(place, level_weights, queries, turned_keys, values, slice_of, done, tree)
        arrived, done = lax.optimization_barrier((arrived, done))
        return arrived, [in_hbm(t) for t in done]

    from_x = swap_three(lambda m: sent[m], "inner", 1)
    from_x, done = beside(from_x, (), 1)
    from_x = [sent[0]] + from_x
    group = from_x[0] + from_x[1] + from_x[2] + from_x[3]

    from_y = swap_three(lambda n: group, "inner", 4)
    from_y, done = beside(from_y, done, 2)
    from_y = [group] + from_y
    block = from_y[0] + from_y[1] + from_y[2] + from_y[3]

    other = swap(block, "outer", 1)
    both = block + other

    from_z = swap_three(lambda n: both, "outer", 2)
    from_z, done = beside(from_z, done, 3)

    upper = picked(y & 1 == 1, ours[7] * from_y[1])
    upper = upper + picked(y >> 1 == 1, ours[8] * (from_y[2] + from_y[3]))
    upper = upper + picked(core == 1, ours[9] * other)
    upper = upper + picked(z & 1 == 1, ours[10] * from_z[0])
    upper = upper + picked(z >> 1 == 1, ours[11] * (from_z[1] + from_z[2]))
    to_x = []
    for m in range(4):
        near = picked((x ^ m) & 1 == 1, ours[5] * from_x[m ^ 1])
        far = picked((x ^ m) >> 1 == 1, ours[6] * (from_x[m ^ 2] + from_x[m ^ 3]))
        to_x.append(near + far + upper)
    trees = swap_three(lambda m: to_x[m], "inner", 1)
    trees, done = beside(trees, done, 0, (to_x[0],))
    return finish(place, *done, trees, out_weight)


def solution(mesh):
    in_specs = (
        P(("outer", "inner"), None),
        P(("outer", "inner"), None),
        P(("outer", "inner"), None),
        P(),
        P(),
    )
    out_specs = P(("outer", "inner"), None)
    return jax.shard_map(per_device, mesh=mesh, in_specs=in_specs, out_specs=out_specs, check_vma=False)
```
